512 devices in a mesh: section: 16 (over y_lo, x, core), dp: 32 (over z, y_hi).
Axes of the slice: x: 4, y: 8 (y_hi: 4, y_lo: 2; y = y_hi * 2 + y_lo), z: 8, core: 2. Of those that a mesh axis runs over, the one named last changes fastest.
Arguments:
- stash: bfloat16 [16, 4096, 2048], P('section', 'dp'), may hold values from -6 to 6
- cotangent: bfloat16 [4096, 2048], P('dp', 'section'), may hold values from -6 to 6
- gate_weight: bfloat16 [16, 2048, 512], P('section', 'dp'), may hold values from -0.125 to 0.125
- up_weight: bfloat16 [16, 2048, 512], P('section', 'dp'), may hold values from -0.125 to 0.125
- down_weight: bfloat16 [16, 512, 2048], P('section'), may hold values from -0.25 to 0.25
- shared_gate: bfloat16 [16, 2048], P('section'), may hold values from -0.125 to 0.125
Outputs:
- grad_inputs: bfloat16 [16, 4096, 2048], P('section', 'dp')
- down_grad: float32 [16, 512, 2048], P('section', 'dp')
The draws below stay inside these ranges and needn't reach their ends.
All inputs are finite; a program needn't handle non-finite values.
Results may differ from the reference program's by a relative error of at most 0.029.
Values may be sent and summed in bfloat16 or wider, within the bound.
A program may use at most 64 MiB of HBM per device.

```python
import jax
import jax.numpy as jnp
from jax import lax

D = 2048
FF = 512
LAYERS = 16
TOKENS = 4096
N_DP = 32


def steps_of(rng, extent, shards, low, largest):
    def one(dim, parts):
        draws = jax.random.uniform(jax.random.fold_in(jax.random.fold_in(rng, 6), dim), (parts,), jnp.float32, low / len(shards), largest / len(shards))
        return jnp.repeat(jnp.exp(draws), extent[dim] // parts).reshape((-1,) + (1,) * (len(extent) - dim - 1))

    gain = one(*shards[0])
    for cut in shards[1:]:
        gain = gain * one(*cut)
    return gain


def bell_draw(own_key, extent, spread, bound, pieces=(), kind=jnp.bfloat16):
    values = spread * jax.random.normal(own_key, extent, jnp.float32)
    if pieces:
        values = values * steps_of(own_key, extent, pieces, -0.22, 0.18)
    return jnp.clip(values, -bound, bound).astype(kind)


def setup_inputs(seed: int = 0) -> dict:
    arg_keys = jax.random.split(jax.random.key(seed), 7)
    stash = bell_draw(arg_keys[0], (LAYERS, TOKENS, D), 1.0, 6.0, ((0, 16), (1, 32)))
    cotangent = bell_draw(arg_keys[1], (TOKENS, D), 1.0, 6.0, ((0, 32), (1, 16)))
    gate_weight = bell_draw(arg_keys[2], (LAYERS, D, FF), D ** -0.5, 0.125, ((0, 16), (1, 32)))
    up_weight = bell_draw(arg_keys[3], (LAYERS, D, FF), D ** -0.5, 0.125, ((0, 16), (1, 32)))
    down_weight = bell_draw(arg_keys[4], (LAYERS, FF, D), FF ** -0.5, 0.25, ((0, 16),))
    shared_gate = bell_draw(arg_keys[5], (LAYERS, D), D ** -0.5, 0.125, ((0, 16),))
    return dict(stash=stash, cotangent=cotangent, gate_weight=gate_weight, up_weight=up_weight, down_weight=down_weight, shared_gate=shared_gate)


def backward_rows(inputs_now, grad_rows, joined, down_full, gate_vector):
    hidden_units = down_full.shape[0]
    projected = jnp.dot(inputs_now, joined, preferred_element_type=jnp.float32)
    gate_pre = projected[:, :hidden_units]
    up_pre = projected[:, hidden_units:]
    gate_score = jax.nn.sigmoid(jnp.dot(inputs_now, gate_vector, preferred_element_type=jnp.float32))[:, None]
    gate_sig = jax.nn.sigmoid(gate_pre)
    activated = gate_pre * gate_sig
    hidden = (activated * up_pre).astype(jnp.bfloat16)
    back_proj = lax.dot_general(grad_rows, down_full, (((1,), (1,)), ((), ())), preferred_element_type=jnp.float32)
    gate_sum = jnp.sum(back_proj * hidden.astype(jnp.float32), axis=1, keepdims=True)
    hidden_grad = gate_score * back_proj
    gate_grad = hidden_grad * up_pre * gate_sig * (1.0 + gate_pre * (1.0 - gate_sig))
    up_grad = hidden_grad * activated
    pair_grad = jnp.concatenate([gate_grad, up_grad], axis=1).astype(jnp.bfloat16)
    through = lax.dot_general(pair_grad, joined, (((1,), (1,)), ((), ())), preferred_element_type=jnp.float32)
    logit_grad = gate_sum * gate_score * (1.0 - gate_score)
    input_grad = (grad_rows.astype(jnp.float32) + through + logit_grad * gate_vector.astype(jnp.float32)[None, :]).astype(jnp.bfloat16)
    scaled = (gate_score * grad_rows.astype(jnp.float32)).astype(jnp.bfloat16)
    return input_grad, hidden, scaled


def replica_sum(group_pair):
    partial_sum = jnp.dot(group_pair[0].T, group_pair[1], preferred_element_type=jnp.float32).astype(jnp.bfloat16)
    return lax.optimization_barrier(partial_sum).astype(jnp.float32)


def reference(stash, cotangent, gate_weight, up_weight, down_weight, shared_gate):
    layer_count = stash.shape[0]
    grad_rows = cotangent
    input_grads = [None] * layer_count
    down_grads = [None] * layer_count
    for layer_index in range(layer_count - 1, -1, -1):
        joined = jnp.concatenate([gate_weight[layer_index], up_weight[layer_index]], axis=1)
        input_grad, hidden, scaled = backward_rows(stash[layer_count - 1 - layer_index], grad_rows, joined, down_weight[layer_index], shared_gate[layer_index])
        groups = (hidden.reshape(N_DP, -1, FF), scaled.reshape(N_DP, -1, D))
        partials = lax.map(replica_sum, groups)
        down_grads[layer_index] = jnp.sum(partials, axis=0) * (TOKENS ** -0.5)
        input_grads[layer_index] = input_grad
        grad_rows = input_grad
    return jnp.stack(input_grads), jnp.stack(down_grads)
```

```python
import functools

import jax
import jax.numpy as jnp
from jax import lax
from jax.experimental import pallas as pl
from jax.experimental.pallas import tpu as pltpu
from jax.sharding import PartitionSpec as P

NY = 4
ROWS = 64
COLS = 512
F32 = jnp.float32
BF16 = jnp.bfloat16
MESH = pl.DeviceIdType.MESH


def nt_dot(a, b):
    return lax.dot_general(a, b, (((1,), (1,)), ((), ())), preferred_element_type=F32)


def kernel(
    sections,
    nz,
    norm,
    stash,
    cot,
    gate,
    up,
    down,
    gvec,
    gi_out,
    dg_out,
    W,
    x,
    wd,
    g,
    o,
    v,
    acc,
    coef,
    hid,
    hid_t,
    gs,
    part,
    rs,
    ys,
    yr,
    dgv,
    loc_sem,
    agy_s,
    agy_r,
    agz_s,
    agz_r,
    st_s,
    st_r,
    cot_s,
    cot_r,
    ch_s,
    ch_r,
    rs_s,
    rs_r,
    y_s,
    y_r,
):
    last = sections - 1
    half = nz // 2
    tokens, width = x.shape
    ff = wd.shape[0]
    zw = width // nz
    piece = zw // NY
    cw = width // sections
    zr = ff // nz
    yrows = zr // NY
    micro = tokens // ROWS
    chunks = width // COLS
    s = lax.axis_index("section")
    dp = lax.axis_index("dp")
    z = lax.div(dp, NY)
    y = lax.rem(dp, NY)
    dirs = (1, -1)
    offs = (0, 1, 3, 2) if NY == 4 else tuple(range(NY))

    def zmod(a):
        return lax.rem(a + 2 * nz, nz)

    def ymod(a):
        return lax.rem(a + NY, NY)

    def at(zz, yy):
        return zz * NY + yy

    def remote(src, dst, ssem, rsem, **where):
        where = {"section": s, "dp": dp, **where}
        return pltpu.make_async_remote_copy(
            src_ref=src,
            dst_ref=dst,
            send_sem=ssem,
            recv_sem=rsem,
            device_id=(where["section"], where["dp"]),
            device_id_type=MESH,
        )

    def in_half(di, j):
        return (j < NY // 2) == (di == 0)

    own = pl.ds(pl.multiple_of(y * piece, piece), piece)
    loads = [
        pltpu.make_async_copy(gate.at[0], W.at[z, 0, own, :], loc_sem.at[0]),
        pltpu.make_async_copy(up.at[0], W.at[z, 1, own, :], loc_sem.at[1]),
        pltpu.make_async_copy(down.at[0], wd, loc_sem.at[2]),
        pltpu.make_async_copy(gvec, v, loc_sem.at[3]),
    ]
    for load in loads:
        load.start()

    barrier = pltpu.get_barrier_semaphore()

    def greet(section, dpi):
        pl.semaphore_signal(barrier, inc=1, device_id=(section, dpi), device_id_type=MESH)

    for dirn in dirs:
        greet(s, at(zmod(z + dirn), y))
    for off in range(1, NY):
        greet(s, at(z, ymod(y + off)))
    greet(last - s, dp)

    @pl.when(s < last)
    def _():
        greet(s + 1, dp)
        greet(last, dp)

    @pl.when(s > 0)
    def _():
        greet(s - 1, dp)

    @pl.when(s == last)
    def _():
        for other in range(last):
            greet(other, dp)

    @pl.when(s == 0)
    def _():
        pl.semaphore_wait(barrier, NY + 2 + 2)

    @pl.when(jnp.logical_and(s > 0, s < last))
    def _():
        pl.semaphore_wait(barrier, NY + 2 + 3)

    @pl.when(s == last)
    def _():
        pl.semaphore_wait(barrier, NY + 2 + 1 + last)

    def wpiece(zz, yy):
        return W.at[zz, :, pl.ds(pl.multiple_of(yy * piece, piece), piece), :]

    def y_copy(off, src_y):
        return remote(
            wpiece(z, src_y),
            wpiece(z, src_y),
            agy_s.at[off - 1],
            agy_r.at[off - 1],
            dp=at(z, ymod(y + off)),
        )

    def z_copy(di, k, j, zo):
        ref = wpiece(zo, ymod(y + offs[j]))
        return remote(
            ref,
            ref,
            agz_s.at[di, k, j],
            agz_r.at[di, k, j],
            dp=at(zmod(z + dirs[di]), y),
        )

    def z_send(di, k, j):
        return z_copy(di, k, j, zmod(z - dirs[di] * k))

    def z_land(di, k, j):
        return z_copy(di, k, j, zmod(z - dirs[di] * (k + 1)))

    stash_copy = remote(stash.at[0], x, st_s, st_r, section=last - s)
    cot_cols = pl.ds(pl.multiple_of(s * cw, cw), cw)
    cot_copy = remote(cot, g.at[:, cot_cols], cot_s, cot_r.at[s], section=last)
    cot_local = pltpu.make_async_copy(cot, g.at[:, cot_cols], cot_s)

    loads[0].wait()
    loads[1].wait()
    for di in range(2):
        z_send(di, 0, 0).start()
    for off in range(1, NY):
        y_copy(off, y).start()
    stash_copy.start()

    @pl.when(s < last)
    def _():
        cot_copy.start()

    @pl.when(s == last)
    def _():
        cot_local.start()

    acc[...] = jnp.zeros_like(acc)
    loads[3].wait()

    def project(zb):
        cols = x[:, pl.ds(pl.multiple_of(zb * zw, zw), zw)]
        for p in range(2):
            acc[:, p * ff : (p + 1) * ff] += jnp.dot(cols, W[zb, p], preferred_element_type=F32)

    events = sorted(
        ((k, j) for k in range(half + 1) for j in range(NY)), key=lambda e: (e[0] + e[1], -e[0])
    )
    for k, j in events:
        if k == 0:
            if j > 0:
                back = NY - offs[j]
                y_copy(back, ymod(y + offs[j])).wait_recv()
                for di in range(2):
                    z_send(di, 0, j).start()
            if j == NY - 1:
                stash_copy.wait_recv()
                project(z)
        else:
            for di in range(2):
                if k < half or in_half(di, j):
                    z_land(di, k - 1, j).wait_recv()
                    if k < half - 1 or (k == half - 1 and in_half(di, j)):
                        z_send(di, k, j).start()
            if j == NY - 1:
                project(zmod(z - k))
                if k < half:
                    project(zmod(z + k))

    vrow = v[...].astype(F32)
    score = jax.nn.sigmoid(jnp.sum(x[...].astype(F32) * vrow, axis=1, keepdims=True))
    gate_pre = acc[:, :ff]
    up_pre = acc[:, ff:]
    sig = jax.nn.sigmoid(gate_pre)
    act = gate_pre * sig
    hidden = (act * up_pre).astype(BF16).astype(F32)
    coef[:, :ff] = score * up_pre * sig * (1.0 + gate_pre * (1.0 - sig))
    coef[:, ff:] = score * act
    hid[...] = hidden
    hid_t[...] = hidden.T.astype(BF16)
    gs[...] = score
    loads[2].wait()

    def chain_copy(m, c):
        ref = (pl.ds(m * ROWS, ROWS), pl.ds(c * COLS, COLS))
        return remote(
            o.at[ref], g.at[ref], ch_s.at[m, c], ch_r.at[m, c], section=lax.max(s - 1, 0)
        )

    @pl.when(s == last)
    def _():
        cot_local.wait()
        for other in range(last):
            cols = pl.ds(other * cw, cw)
            remote(cot, g.at[:, cols], cot_s, cot_r.at[other], section=last).wait_recv()

    for m in range(micro):
        rows = pl.ds(m * ROWS, ROWS)
        back_proj = jnp.zeros((ROWS, ff), F32)
        for c in range(chunks):
            cols = pl.ds(c * COLS, COLS)

            @pl.when(s < last)
            def _():
                chain_copy(m, c).wait_recv()

            back_proj += nt_dot(g[rows, cols], wd[:, cols])
        gate_grad = (back_proj * coef[rows, :ff]).astype(BF16)
        up_grad = (back_proj * coef[rows, ff:]).astype(BF16)
        row_score = gs[rows, :]
        logit = jnp.sum(back_proj * hid[rows, :], axis=1, keepdims=True)
        logit = logit * row_score * (1.0 - row_score)
        for c in range(chunks):
            for b in range(COLS // zw):
                zb = c * (COLS // zw) + b
                cols = pl.ds(zb * zw, zw)
                through = nt_dot(gate_grad, W[zb, 0]) + nt_dot(up_grad, W[zb, 1])
                total = g[rows, cols].astype(F32) + through
                total = total + logit * v[:, cols].astype(F32)
                o[rows, cols] = total.astype(BF16)

            @pl.when(s > 0)
            def _():
                chain_copy(m, c).start()

    gi_copy = pltpu.make_async_copy(o, gi_out, loc_sem.at[0])
    gi_copy.start()

    x[...] = (gs[...] * g[...].astype(F32)).astype(BF16)

    def block(zz):
        start = pl.multiple_of(zz * zr, zr)
        rows = pl.ds(start, zr)
        part[rows, :] = jnp.dot(hid_t[rows, :], x[...], preferred_element_type=F32).astype(BF16)

    def sub(zz, j):
        return pl.ds(pl.multiple_of(zz * zr + ymod(y + offs[j]) * yrows, yrows), yrows)

    def lane(j):
        return pl.ds(pl.multiple_of(ymod(y + offs[j]) * yrows, yrows), yrows)

    def rs_copy(di, d, j):
        return remote(
            part.at[sub(zmod(z + dirs[di] * d), j), :],
            rs.at[di, d - 1, lane(j), :],
            rs_s.at[di, d - 1, j],
            rs_r.at[di, d - 1, j],
            dp=at(zmod(z + dirs[di]), y),
        )

    order = tuple(range(NY - 1, -1, -1))
    block(zmod(z + half))
    for j in order:
        for di in range(2):
            if in_half(di, j):
                rs_copy(di, half, j).start()
    for d in range(half - 1, 0, -1):
        for di in range(2):
            block(zmod(z + dirs[di] * d))
        for di in range(2):
            js = order
            if d == half - 1:
                js = [j for j in order if not in_half(di, j)] + [j for j in order if in_half(di, j)]
            for j in js:
                if d < half - 1 or in_half(di, j):
                    rs_copy(di, d + 1, j).wait_recv()
                    rows = sub(zmod(z + dirs[di] * d), j)
                    total = part[rows, :].astype(F32) + rs[di, d, lane(j), :].astype(F32)
                    part[rows, :] = total.astype(BF16)
                rs_copy(di, d, j).start()
    block(z)

    def y_sum_copy(off):
        return remote(
            ys.at[off - 1], yr.at[off - 1], y_s.at[off - 1], y_r.at[off - 1], dp=at(z, ymod(y + off))
        )

    for j in order:
        total = part[sub(z, j), :].astype(F32)
        for di in range(2):
            rs_copy(di, 1, j).wait_recv()
            total = total + rs[di, 0, lane(j), :].astype(F32)
        if offs[j] == 0:
            dgv[...] = total
        else:
            ys[offs[j] - 1] = total.astype(BF16)
            y_sum_copy(offs[j]).start()
    total = dgv[...]
    for off in range(1, NY):
        y_sum_copy(off).wait_recv()
        total = total + yr[off - 1].astype(F32)
    dgv[...] = total * norm
    dg_copy = pltpu.make_async_copy(dgv, dg_out, loc_sem.at[1])
    dg_copy.start()

    for off in range(1, NY):
        y_copy(off, y).wait_send()
        y_sum_copy(off).wait_send()
    for di in range(2):
        for j in range(NY):
            for k in range(half):
                if k < half - 1 or in_half(di, j):
                    z_send(di, k, j).wait_send()
                    rs_copy(di, k + 1, j).wait_send()
    stash_copy.wait_send()

    @pl.when(s < last)
    def _():
        cot_copy.wait_send()

    @pl.when(s > 0)
    def _():
        for m in range(micro):
            for c in range(chunks):
                chain_copy(m, c).wait_send()

    gi_copy.wait()
    dg_copy.wait()


def on_device(sections, nz, stash, cotangent, gate_weight, up_weight, down_weight, shared_gate):
    tokens, width = stash.shape[1:]
    ff = down_weight.shape[1]
    half = nz // 2
    zr = ff // nz
    yrows = zr // NY
    micro = tokens // ROWS
    chunks = width // COLS
    norm = (tokens * nz * NY) ** (-0.5)
    dma = pltpu.SemaphoreType.DMA
    hbm = pl.BlockSpec(memory_space=pl.ANY)
    results, grad = pl.pallas_call(
        functools.partial(kernel, sections, nz, norm),
        out_shape=(
            jax.ShapeDtypeStruct((tokens, width), BF16),
            jax.ShapeDtypeStruct((yrows, width), F32),
        ),
        in_specs=[hbm] * 6,
        out_specs=(hbm, hbm),
        scratch_shapes=[
            pltpu.VMEM((nz, 2, width // nz, ff), BF16),
            pltpu.VMEM((tokens, width), BF16),
            pltpu.VMEM((ff, width), BF16),
            pltpu.VMEM((tokens, width), BF16),
            pltpu.VMEM((tokens, width), BF16),
            pltpu.VMEM((1, width), BF16),
            pltpu.VMEM((tokens, 2 * ff), F32),
            pltpu.VMEM((tokens, 2 * ff), F32),
            pltpu.VMEM((tokens, ff), F32),
            pltpu.VMEM((ff, tokens), BF16),
            pltpu.VMEM((tokens, 1), F32),
            pltpu.VMEM((ff, width), BF16),
            pltpu.VMEM((2, half, zr, width), BF16),
            pltpu.VMEM((NY - 1, yrows, width), BF16),
            pltpu.VMEM((NY - 1, yrows, width), BF16),
            pltpu.VMEM((yrows, width), F32),
            dma((4,)),
            dma((NY - 1,)),
            dma((NY - 1,)),
            dma((2, half, NY)),
            dma((2, half, NY)),
            dma,
            dma,
            dma,
            dma((sections,)),
            dma((micro, chunks)),
            dma((micro, chunks)),
            dma((2, half, NY)),
            dma((2, half, NY)),
            dma((NY - 1,)),
            dma((NY - 1,)),
        ],
        compiler_params=pltpu.CompilerParams(
            collective_id=0, has_side_effects=True, vmem_limit_bytes=48 * 2**20
        ),
        name="chain",
    )(stash, cotangent, gate_weight, up_weight, down_weight, shared_gate)
    return results[None], grad[None]


def solution(mesh):
    placed = (
        P("section", "dp", None),
        P("dp", "section"),
        P("section", "dp", None),
        P("section", "dp", None),
        P("section", None, None),
        P("section", None),
    )
    return jax.shard_map(
        functools.partial(on_device, mesh.shape["section"], mesh.shape["dp"] // NY),
        mesh=mesh,
        in_specs=placed,
        out_specs=(P("section", "dp", None), P("section", "dp", None)),
        check_vma=False,
    )
```
